256 devices in a mesh: walk: 128 (over x, z, y), tan: 2 (over core).
Axes of the slice: x: 4, y: 4, z: 8, core: 2. Of those that a mesh axis runs over, the one named last changes fastest.
Arguments:
- values: bfloat16 [512, 64, 256], P('walk', 'tan'), may hold values from -6 to 6
- lap_in: bfloat16 [512, 64, 256], P('walk', 'tan'), may hold values from -6 to 6
- tangent: bfloat16 [512, 192, 64, 256], P('walk', None, 'tan'), may hold values from -0.4375 to 0.4375
- slot_electron: int32 [512, 64], P('walk'), may hold values from 0 to 63, each once within a row
- spin_up: int32 [512], P('walk'), may hold values from 16 to 48
- w_self: bfloat16 [256, 256], replicated, may hold values from -0.375 to 0.375
- w_spin: bfloat16 [256, 256], replicated, may hold values from -1.5 to 1.5
- bias: float32 [256], replicated, may hold values from -3 to 3
- readout: float32 [256], replicated, may hold values from -0.046875 to 0.046875
- potential: float32 [512], P('walk'), may hold values from -6 to 6
Outputs:
- laplacian: float32 [512, 64, 256], P('walk', 'tan')
- energy: float32 [512], P('walk')
- grad_self: float32 [256, 256], replicated
- grad_spin: float32 [256, 256], replicated
The draws below stay inside these ranges and needn't reach their ends.
Inputs may be any that keep to these rules, and one draw needn't show every extreme that they name: `slot_electron`: each walker's row names every electron once.
All inputs are finite; a program needn't handle non-finite values.
Results may differ from the reference program's by a relative error of at most 0.004.
Values may be sent and summed in bfloat16 or wider, within the bound.
A program may use at most 64 MiB of HBM per device.

```python
import jax
import jax.numpy as jnp
from jax import lax

FEAT = 256
ELEC = 64
DIRS = 192
WALKERS = 512


def set_ends(drawn, own_key, smallest, high):
    longest = drawn.shape.index(max(drawn.shape))
    spots = []
    for shift in (0, 1):
        where = [jax.random.randint(jax.random.fold_in(own_key, axis), (), 0, length) for axis, length in enumerate(drawn.shape)]
        where[longest] = (where[longest] + shift) % drawn.shape[longest]
        spots.append(tuple(where))
    return drawn.at[spots[0]].set(smallest).at[spots[1]].set(high)


def levels(stream_key, dims, split, smallest, high):
    loudness, own = 1.0, jax.random.fold_in(stream_key, 6)
    for position, parts in split:
        draws = jnp.exp(jax.random.uniform(jax.random.fold_in(own, position), (parts,), jnp.float32, smallest / len(split), high / len(split)))
        loudness = loudness * jnp.repeat(draws, dims[position] // parts).reshape([-1 if axis == position else 1 for axis in range(len(dims))])
    return loudness


def gaussian(key, shape, scale, bound, pieces=(), kind=jnp.bfloat16):
    drawn = jax.random.normal(key, shape, jnp.float32) * scale
    if len(pieces) > 0:
        drawn = levels(key, shape, pieces, -0.22, 0.18) * drawn
    return jnp.clip(drawn, min=-bound, max=bound).astype(kind)


def setup_inputs(seed: int = 0) -> dict:
    key_list = jax.random.split(jax.random.key(seed), 11)
    values = gaussian(key_list[0], (WALKERS, ELEC, FEAT), 1.0, 6.0, ((0, 128), (1, 2)))
    lap_in = gaussian(key_list[1], (WALKERS, ELEC, FEAT), 1.0, 6.0, ((0, 128), (1, 2)))
    tangent = gaussian(key_list[2], (WALKERS, DIRS, ELEC, FEAT), DIRS ** -0.5, 0.4375, ((0, 128), (2, 2)))
    slot_electron = jax.vmap(lambda own: jax.random.permutation(own, ELEC))(jax.random.split(key_list[3], WALKERS)).reshape((WALKERS, ELEC)).astype(jnp.int32)
    spin_up = set_ends(jax.random.randint(key_list[4], (WALKERS,), ELEC // 4, 3 * ELEC // 4 + 1), jax.random.fold_in(key_list[4], 1), ELEC // 4, (3 * ELEC // 4 + 1) - 1).astype(jnp.int32)
    w_self = gaussian(key_list[5], (FEAT, FEAT), FEAT ** -0.5, 0.375)
    w_spin = gaussian(key_list[6], (FEAT, FEAT), 0.25, 1.5)
    bias = gaussian(key_list[7], (FEAT,), 0.5, 3.0, (), jnp.float32)
    readout = gaussian(key_list[8], (FEAT,), (ELEC * FEAT) ** -0.5, 0.046875, (), jnp.float32)
    potential = gaussian(key_list[9], (WALKERS,), 1.0, 6.0, ((0, 128),), jnp.float32)
    return dict(values=values, lap_in=lap_in, tangent=tangent, slot_electron=slot_electron, spin_up=spin_up, w_self=w_self, w_spin=w_spin, bias=bias, readout=readout, potential=potential)


def pick_spin(upper_spin, mixed_rows):
    return upper_spin[..., :, None] * mixed_rows[..., 0:1, :] + (1.0 - upper_spin[..., :, None]) * mixed_rows[..., 1:2, :]


def one_walker(walker_items, w_self, w_spin, bias, readout):
    feats, lap_feats, tangent_block, mask_rows, count_row, upper_spin, pot_value = walker_items
    mask_bf = mask_rows.astype(jnp.bfloat16)
    mean_values = (jnp.dot(mask_bf, feats, preferred_element_type=jnp.float32) / count_row[:, None]).astype(jnp.bfloat16)
    mean_lap = (jnp.dot(mask_bf, lap_feats, preferred_element_type=jnp.float32) / count_row[:, None]).astype(jnp.bfloat16)
    preact = jnp.dot(feats, w_self, preferred_element_type=jnp.float32) + pick_spin(upper_spin, jnp.dot(mean_values, w_spin, preferred_element_type=jnp.float32)) + bias
    lap_pre = jnp.dot(lap_feats, w_self, preferred_element_type=jnp.float32) + pick_spin(upper_spin, jnp.dot(mean_lap, w_spin, preferred_element_type=jnp.float32))
    squash = jnp.tanh(preact)
    slopes = 1.0 - squash * squash
    curvature = -2.0 * squash * slopes
    spin_sums = jnp.einsum("se,def->dsf", mask_rows.astype(jnp.float32), tangent_block.astype(jnp.float32), precision=lax.Precision.HIGHEST)
    spin_means = (spin_sums / count_row[None, :, None]).astype(jnp.bfloat16)
    dirs_count = tangent_block.shape[0]
    feat_width = tangent_block.shape[2]
    mixed_rows = jnp.dot(spin_means.reshape(-1, feat_width), w_spin, preferred_element_type=jnp.float32).reshape(dirs_count, 2, feat_width)
    change = jnp.dot(tangent_block.reshape(-1, feat_width), w_self, preferred_element_type=jnp.float32).reshape(tangent_block.shape) + pick_spin(upper_spin, mixed_rows)
    squares = jnp.sum(change * change, axis=0)
    weighted_slope = slopes * readout
    gradient = jnp.einsum("def,ef->d", change, weighted_slope, precision=lax.Precision.HIGHEST)
    laplacian = slopes * lap_pre + curvature * squares
    lap_sum = jnp.sum(laplacian * readout)
    energy = -0.5 * (lap_sum + jnp.sum(gradient * gradient)) + pot_value
    slope_bf = weighted_slope.astype(jnp.bfloat16)
    picked = pick_spin(upper_spin, mean_values.astype(jnp.float32)).astype(jnp.bfloat16)
    first_terms = jnp.dot(feats.T, slope_bf, preferred_element_type=jnp.float32)
    spin_terms = jnp.dot(picked.T, slope_bf, preferred_element_type=jnp.float32)
    return laplacian, energy, first_terms, spin_terms


def reference(values, lap_in, tangent, slot_electron, spin_up, w_self, w_spin, bias, readout, potential):
    upper_spin = (slot_electron < spin_up[:, None]).astype(jnp.float32)
    mask_rows = jnp.stack([upper_spin, 1.0 - upper_spin], axis=1)
    up_count = spin_up.astype(jnp.float32)
    count_rows = jnp.stack([up_count, ELEC - up_count], axis=1)
    laplacian, energy, first_terms, spin_terms = lax.map(
        lambda walker_items: one_walker(walker_items, w_self, w_spin, bias, readout),
        (values, lap_in, tangent, mask_rows, count_rows, upper_spin, potential))
    center = jnp.sum(energy) / WALKERS
    spread = energy - center
    grad_self = jnp.einsum("w,wfg->fg", spread, first_terms, precision=lax.Precision.HIGHEST)
    grad_spin = jnp.einsum("w,wfg->fg", spread, spin_terms, precision=lax.Precision.HIGHEST)
    return laplacian, energy, grad_self, grad_spin
```

```python
import jax
import jax.numpy as jnp
from jax import lax
from jax.experimental import pallas as pl
from jax.experimental.pallas import tpu as pltpu
from jax.sharding import PartitionSpec as P

MESH = pl.DeviceIdType.MESH
F32 = jnp.float32
BF16 = jnp.bfloat16
NX, NZ, NY = 4, 8, 4
XY = NX * NY
BLOCK = 8


def iota(shape, axis):
    return lax.broadcasted_iota(jnp.int32, shape, axis)


def dot(a, b):
    return jnp.dot(a, b, preferred_element_type=F32)


def body(
    values, lap_in, tangent, slots, spin, w_self, w_spin, bias, readout, potential,
    lap_out, energy_out, grads_out,
    full_v, full_l, tan, own_sums, got_sums, mixed, sel, terms, slopes_s, lap_pre_s,
    partial, own_ex, got_ex, shard_s, recv_s, mine_s, zs, shard_e, recv_e, mine_e, ze,
    load_sem, tan_sem, pair_send, pair_recv,
    rs_send, rs_recv, z_send, z_recv, ag_send, ag_recv,
):
    walkers, dirs, own, feat = tangent.shape
    elec = slots.shape[1]
    rows = BLOCK * own
    blocks = dirs // BLOCK
    me = lax.axis_index("walk")
    core = lax.axis_index("tan")
    x = me // (NZ * NY)
    z = (me // NY) % NZ
    y = me % NY
    here = x * NY + y
    partner = (me, 1 - core)

    def across(k):
        px = (x + k // NY) % NX
        py = (y + k % NY) % NY
        return (px * NZ + z) * NY + py, px * NY + py

    def behind(k):
        return ((x - k // NY + NX) % NX) * NY + (y - k % NY + NY) % NY

    def along(k):
        return (x * NZ + (z + k) % NZ) * NY + y

    off = pl.multiple_of(core * own, own)
    load_v = pltpu.make_async_copy(values, full_v.at[:, pl.ds(off, own)], load_sem.at[0])
    load_l = pltpu.make_async_copy(lap_in, full_l.at[:, pl.ds(off, own)], load_sem.at[1])
    for w in range(walkers):
        pltpu.make_async_copy(tangent.at[w], tan.at[w], tan_sem.at[w]).start()
        if w == 0:
            load_v.start()
            load_l.start()

    barrier = pltpu.get_barrier_semaphore()
    pl.semaphore_signal(barrier, inc=1, device_id=partner, device_id_type=MESH)

    def greet(k, carry):
        to, _ = across(k)
        for other in (core, 1 - core):
            pl.semaphore_signal(barrier, inc=1, device_id=(to, other), device_id_type=MESH)
        return carry

    def greet_z(k, carry):
        pl.semaphore_signal(barrier, inc=1, device_id=(along(k), core), device_id_type=MESH)
        return carry

    lax.fori_loop(1, XY, greet, 0)
    lax.fori_loop(1, NZ, greet_z, 0)

    s8 = jnp.concatenate([slots[...]] * (8 // walkers), 0)
    r8 = iota((8, elec), 0) % walkers
    n8 = jnp.zeros((8, elec), jnp.int32)
    for w in range(walkers):
        n8 = jnp.where(r8 == w, spin[w], n8)
    upper = (s8 < n8).astype(F32).astype(BF16)
    spread = (iota((elec, rows), 0) == core * own + iota((elec, rows), 1) % own).astype(F32)
    tiled = dot(upper, spread.astype(BF16))
    eye = (iota((elec, elec), 0) == iota((elec, elec), 1)).astype(F32).astype(BF16)
    columns = lax.dot_general(eye, upper, (((1,), (1,)), ((), ())), preferred_element_type=F32)
    own_eye = (iota((own, elec), 0) + core * own == iota((own, elec), 1)).astype(F32).astype(BF16)
    own_columns = lax.dot_general(
        own_eye, upper, (((1,), (1,)), ((), ())), preferred_element_type=F32
    )
    r16 = iota((2 * BLOCK, rows), 0)
    c16 = iota((2 * BLOCK, rows), 1)
    for w in range(walkers):
        m = tiled[w : w + 1]
        m = jnp.where(r16 < BLOCK, m, 1.0 - m)
        sel[w] = jnp.where(c16 // own == r16 % BLOCK, m, 0.0).astype(BF16)

    def group_sums(w):
        pick = sel[w]

        def step(i, carry):
            d = pl.multiple_of(i * BLOCK, BLOCK)
            t = tan[w, pl.ds(d, BLOCK)].reshape(rows, feat)
            r = dot(pick, t)
            own_sums[w, 0, pl.ds(d, BLOCK)] = r[:BLOCK]
            own_sums[w, 1, pl.ds(d, BLOCK)] = r[BLOCK:]
            return carry

        lax.fori_loop(0, blocks, step, 0, unroll=4)

    def sums_copy(w):
        return pltpu.make_async_remote_copy(
            src_ref=own_sums.at[w],
            dst_ref=got_sums.at[w],
            send_sem=pair_send.at[w],
            recv_sem=pair_recv.at[w],
            device_id=partner,
            device_id_type=MESH,
        )

    def tan_wait(w):
        pltpu.make_async_copy(tangent.at[w], tan.at[w], tan_sem.at[w]).wait()

    tan_wait(0)
    group_sums(0)
    pl.semaphore_wait(barrier, 1 + 2 * (XY - 1) + NZ - 1)

    def to_partner(src, dst, i):
        return pltpu.make_async_remote_copy(
            src_ref=src,
            dst_ref=dst,
            send_sem=pair_send.at[i],
            recv_sem=pair_recv.at[i],
            device_id=partner,
            device_id_type=MESH,
        )

    send_v = to_partner(values, full_v.at[:, pl.ds(off, own)], walkers)
    send_l = to_partner(lap_in, full_l.at[:, pl.ds(off, own)], walkers + 1)
    send_v.start()
    send_l.start()
    sums_copy(0).start()
    for w in range(1, walkers):
        tan_wait(w)
        group_sums(w)
        sums_copy(w).start()
    load_v.wait()
    load_l.wait()
    send_v.wait()
    send_l.wait()

    gain = readout[...].reshape(1, feat)
    shift = bias[...].reshape(1, feat)
    row8 = iota((8, elec), 0)
    row81 = iota((8, 1), 0)
    total = jnp.zeros((feat, feat), F32)
    for w in range(walkers):
        n0 = spin[w].astype(F32)
        n1 = elec - n0
        up = upper[w : w + 1].astype(F32)
        masks = jnp.where(row8 == 0, up, jnp.where(row8 == 1, 1.0 - up, 0.0)).astype(BF16)
        counts = jnp.where(row81 == 0, n0, jnp.where(row81 == 1, n1, 1.0))
        mean_v = (dot(masks, full_v[w]) / counts).astype(BF16)
        mean_l = (dot(masks, full_l[w]) / counts).astype(BF16)
        mix_v = dot(mean_v, w_spin[...])
        mix_l = dot(mean_l, w_spin[...])
        is_up = columns[:, w : w + 1] > 0.5
        own_up = own_columns[:, w : w + 1] > 0.5
        pre = dot(full_v[w], w_self[...]) + jnp.where(is_up, mix_v[0:1], mix_v[1:2]) + shift
        squash = jnp.tanh(pre)
        slopes = 1.0 - squash * squash
        slopes_s[0, w] = slopes
        slopes_s[1, w] = -2.0 * squash * slopes
        lap_own = full_l[w, pl.ds(off, own)]
        lap_pre_s[w] = dot(lap_own, w_self[...]) + jnp.where(own_up, mix_l[0:1], mix_l[1:2])
        slope_bf = (slopes * gain).astype(BF16)
        mean_f = mean_v.astype(F32)
        picked = jnp.where(is_up, mean_f[0:1], mean_f[1:2])
        left = jnp.where(core == 0, full_v[w].astype(F32), picked).astype(BF16)
        term = lax.dot_general(
            left, slope_bf, (((0,), (0,)), ((), ())), preferred_element_type=F32
        )
        terms[w] = term
        total = total + term
    per = feat // XY
    shard_s[...] = total.reshape(XY, per, feat)

    def scatter(src, dst, send, recv):
        dst[here] = src[here]

        def go(k, carry):
            to, slot = across(k)
            pltpu.make_async_remote_copy(
                src_ref=src.at[slot],
                dst_ref=dst.at[here],
                send_sem=send.at[k],
                recv_sem=recv.at[k],
                device_id=(to, core),
                device_id_type=MESH,
            ).start()
            return carry

        lax.fori_loop(1, XY, go, 0)

    def scatter_wait(src, dst, send, recv):
        def go(k, carry):
            to, slot = across(k)
            pltpu.make_async_remote_copy(
                src_ref=src.at[slot],
                dst_ref=dst.at[behind(k)],
                send_sem=send.at[k],
                recv_sem=recv.at[k],
                device_id=(to, core),
                device_id_type=MESH,
            ).wait()
            return carry

        lax.fori_loop(1, XY, go, 0)

    def over_z(src, dst, send, recv):
        dst[z] = src[...]
        for k in range(1, NZ):
            pltpu.make_async_remote_copy(
                src_ref=src,
                dst_ref=dst.at[z],
                send_sem=send.at[k],
                recv_sem=recv.at[k],
                device_id=(along(k), core),
                device_id_type=MESH,
            ).start()

    def over_z_wait(src, dst, send, recv):
        for k in range(1, NZ):
            pltpu.make_async_remote_copy(
                src_ref=src,
                dst_ref=dst.at[(z - k + NZ) % NZ],
                send_sem=send.at[k],
                recv_sem=recv.at[k],
                device_id=(along(k), core),
                device_id_type=MESH,
            ).wait()

    def add_up(ref, n):
        acc = ref[0]
        for j in range(1, n):
            acc = acc + ref[j]
        return acc

    scatter(shard_s, recv_s, rs_send.at[0], rs_recv.at[0])

    partial[dirs + 1 : dirs + 8] = jnp.zeros((7, 8, 128), F32)
    ones = jnp.ones((8, 128), F32)
    own_ex[...] = jnp.zeros((8, 256), F32)
    for w in range(walkers):
        sums_copy(w).wait()
        n0 = spin[w].astype(F32)
        inv = 1.0 / jnp.concatenate(
            [jnp.full((1, 1, 1), n0, F32), jnp.full((1, 1, 1), elec - n0, F32)], 0
        )
        means = ((own_sums[w] + got_sums[w]) * inv).astype(BF16)
        mixed[...] = dot(means.reshape(2 * dirs, feat), w_spin[...]).reshape(2, dirs, feat)
        own_up = jnp.broadcast_to(own_columns[:, w : w + 1], (own, feat)) > 0.5
        own_slopes = slopes_s[0, w, pl.ds(off, own)]
        own_curve = slopes_s[1, w, pl.ds(off, own)]
        weighted = own_slopes * gain

        def step(i, acc):
            d = pl.multiple_of(i * BLOCK, BLOCK)
            t = tan[w, pl.ds(d, BLOCK)].reshape(rows, feat)
            a = dot(t, w_self[...])
            for j in range(BLOCK):
                m0 = mixed[0, pl.ds(d + j, 1)]
                m1 = mixed[1, pl.ds(d + j, 1)]
                ch = a[j * own : (j + 1) * own] + jnp.where(own_up, m0, m1)
                acc = acc + ch * ch
                p = (ch * weighted).reshape(own // 8, 8, feat).sum(axis=0)
                partial[d + j] = p[:, :128] + p[:, 128:]
            return acc

        squares = lax.fori_loop(0, blocks, step, jnp.zeros((own, feat), F32))
        lap = own_slopes * lap_pre_s[w] + own_curve * squares
        lap_out[w] = lap
        lp = (lap * gain).reshape(own // 8, 8, feat).sum(axis=0)
        partial[dirs] = lp[:, :128] + lp[:, 128:]
        g = jnp.concatenate(
            [partial[...].sum(axis=1), jnp.zeros((256 - dirs - 8, 128), F32)], 0
        )
        g = lax.dot_general(
            ones, g, (((1,), (1,)), ((), ())),
            precision=lax.Precision.HIGHEST, preferred_element_type=F32,
        )
        own_ex[...] = jnp.where(iota((8, 256), 0) == w, g, own_ex[...])
        if w == 1:
            scatter_wait(shard_s, recv_s, rs_send.at[0], rs_recv.at[0])
            mine_s[...] = add_up(recv_s, XY)
            over_z(mine_s, zs, z_send.at[0], z_recv.at[0])

    ex = to_partner(own_ex, got_ex, walkers + 2)
    ex.start()
    ex.wait()
    both = own_ex[...] + got_ex[...]
    lane = iota((8, 256), 1)
    both = jnp.where(lane < dirs, both * both, jnp.where(lane == dirs, both, 0.0))
    pot = jnp.zeros((8, 1), F32)
    for w in range(walkers):
        pot = jnp.where(row81 == w, potential[w], pot)
    energy = -0.5 * jnp.sum(both, axis=1, keepdims=True) + pot
    energy_out[...] = jnp.broadcast_to(energy, (8, 128))
    esum = jnp.broadcast_to(jnp.sum(energy, axis=0, keepdims=True), (8, feat))

    grad = energy[0:1] * terms[0]
    for w in range(1, walkers):
        grad = grad + energy[w : w + 1] * terms[w]
    shard_e[:, :per] = grad.reshape(XY, per, feat)
    shard_e[:, per:] = jnp.broadcast_to(esum[None], (XY, 8, feat))
    scatter(shard_e, recv_e, rs_send.at[1], rs_recv.at[1])
    over_z_wait(mine_s, zs, z_send.at[0], z_recv.at[0])
    plain = add_up(zs, NZ)
    scatter_wait(shard_e, recv_e, rs_send.at[1], rs_recv.at[1])
    mine_e[...] = add_up(recv_e, XY)
    over_z(mine_e, ze, z_send.at[1], z_recv.at[1])
    over_z_wait(mine_e, ze, z_send.at[1], z_recv.at[1])
    summed = add_up(ze, NZ)
    center = summed[per : per + 1] / (walkers * NX * NY * NZ)
    grads_out[core, here] = (summed[:per] - center * plain).astype(BF16)

    def gather_copy(k, other, matrix, slot, i):
        to, _ = across(k)
        return pltpu.make_async_remote_copy(
            src_ref=grads_out.at[core, here],
            dst_ref=grads_out.at[matrix, slot],
            send_sem=ag_send.at[i, k],
            recv_sem=ag_recv.at[i, k],
            device_id=(to, other),
            device_id_type=MESH,
        )

    def gather(k, carry):
        gather_copy(k, core, core, here, 0).start()
        gather_copy(k, 1 - core, core, here, 1).start()
        return carry

    def gather_wait(k, carry):
        gather_copy(k, core, core, behind(k), 0).wait()
        gather_copy(k, 1 - core, 1 - core, behind(k), 1).wait()
        return carry

    gather_copy(0, 1 - core, core, here, 1).start()
    lax.fori_loop(1, XY, gather, 0)
    gather_copy(0, 1 - core, 1 - core, here, 1).wait()
    lax.fori_loop(1, XY, gather_wait, 0)


def shards(
    values, lap_in, tangent, slot_electron, spin_up, w_self, w_spin, bias, readout, potential
):
    walkers, dirs, own, feat = tangent.shape
    elec = slot_electron.shape[1]
    per = feat // XY
    vmem = pl.BlockSpec(memory_space=pltpu.VMEM)
    smem = pl.BlockSpec(memory_space=pltpu.SMEM)
    hbm = pl.BlockSpec(memory_space=pl.ANY)
    dma = pltpu.SemaphoreType.DMA
    lap, energy, grads = pl.pallas_call(
        body,
        out_shape=(
            jax.ShapeDtypeStruct((walkers, own, feat), F32),
            jax.ShapeDtypeStruct((8, 128), F32),
            jax.ShapeDtypeStruct((2, XY, per, feat), BF16),
        ),
        in_specs=[hbm, hbm, hbm, vmem, smem, vmem, vmem, vmem, vmem, smem],
        out_specs=(vmem, vmem, vmem),
        scratch_shapes=[
            pltpu.VMEM((walkers, elec, feat), BF16),
            pltpu.VMEM((walkers, elec, feat), BF16),
            pltpu.VMEM((walkers, dirs, own, feat), BF16),
            pltpu.VMEM((walkers, 2, dirs, feat), F32),
            pltpu.VMEM((walkers, 2, dirs, feat), F32),
            pltpu.VMEM((2, dirs, feat), F32),
            pltpu.VMEM((walkers, 2 * BLOCK, BLOCK * own), BF16),
            pltpu.VMEM((walkers, feat, feat), F32),
            pltpu.VMEM((2, walkers, elec, feat), F32),
            pltpu.VMEM((walkers, own, feat), F32),
            pltpu.VMEM((dirs + 8, 8, 128), F32),
            pltpu.VMEM((8, 256), F32),
            pltpu.VMEM((8, 256), F32),
            pltpu.VMEM((XY, per, feat), F32),
            pltpu.VMEM((XY, per, feat), F32),
            pltpu.VMEM((per, feat), F32),
            pltpu.VMEM((NZ, per, feat), F32),
            pltpu.VMEM((XY, per + 8, feat), F32),
            pltpu.VMEM((XY, per + 8, feat), F32),
            pltpu.VMEM((per + 8, feat), F32),
            pltpu.VMEM((NZ, per + 8, feat), F32),
            dma((2,)),
            dma((walkers,)),
            dma((walkers + 3,)),
            dma((walkers + 3,)),
            dma((2, XY)),
            dma((2, XY)),
            dma((2, NZ)),
            dma((2, NZ)),
            dma((2, XY)),
            dma((2, XY)),
        ],
        compiler_params=pltpu.CompilerParams(
            collective_id=0, has_side_effects=True, vmem_limit_bytes=60 << 20
        ),
        name="forward_laplacian",
    )(values, lap_in, tangent, slot_electron, spin_up, w_self, w_spin, bias, readout, potential)
    grads = grads.astype(F32).reshape(2, feat, feat)
    return lap, energy[:walkers, 0], grads[0], grads[1]


def solution(mesh):
    placed = (
        P("walk", "tan", None),
        P("walk", "tan", None),
        P("walk", None, "tan", None),
        P("walk", None),
        P("walk"),
        P(),
        P(),
        P(),
        P(),
        P("walk"),
    )
    return jax.shard_map(
        shards,
        mesh=mesh,
        in_specs=placed,
        out_specs=(P("walk", "tan", None), P("walk"), P(), P()),
        check_vma=False,
    )
```

```python
import jax
import jax.numpy as jnp
from jax import lax
from jax.experimental import pallas as pl
from jax.experimental.pallas import tpu as pltpu
from jax.sharding import PartitionSpec as P

MESH = pl.DeviceIdType.MESH
F32 = jnp.float32
BF16 = jnp.bfloat16
NX, NZ, NY = 4, 8, 4
XY = NX * NY
BLOCK = 8
STAGE = 32


def iota(shape, axis):
    return lax.broadcasted_iota(jnp.int32, shape, axis)


def dot(a, b):
    return jnp.dot(a, b, preferred_element_type=F32)


def body(
    values, lap_in, tangent, slots, spin, w_self, w_spin, bias, readout, potential,
    lap_out, energy_out, grads_out,
    full_v, full_l, tan, own_sums, got_sums, mixed, sel, terms, slopes_s, lap_pre_s,
    partial, prod_a, prod_b, part_a, part_b, own_ex, got_ex, shard_s, recv_s, mine_s, zs, shard_e, recv_e, mine_e, ze,
    own_e, plane_e, mine_z, all_e,
    load_sem, tan_sem, pair_send, pair_recv,
    rs_send, rs_recv, z_send, z_recv, ag_send, ag_recv,
):
    walkers, dirs, own, feat = tangent.shape
    elec = slots.shape[1]
    rows = BLOCK * own
    blocks = dirs // BLOCK
    me = lax.axis_index("walk")
    core = lax.axis_index("tan")
    x = lax.div(me, NZ * NY)
    z = lax.rem(lax.div(me, NY), NZ)
    y = lax.rem(me, NY)
    here = x * NY + y
    partner = (me, 1 - core)
    xs = [x] + [lax.rem(x + i, NX) for i in range(1, NX)]
    ys = [y] + [lax.rem(y + i, NY) for i in range(1, NY)]
    lines = [xs[i] * (NZ * NY) + z * NY for i in range(NX)]
    columns_z = [me] + [x * (NZ * NY) + lax.rem(z + i, NZ) * NY + y for i in range(1, NZ)]

    def across(k):
        return lines[k // NY] + ys[k % NY], xs[k // NY] * NY + ys[k % NY]

    def behind(k):
        return xs[-(k // NY) % NX] * NY + ys[-(k % NY) % NY]

    def along(k):
        return columns_z[k]

    off = pl.multiple_of(core * own, own)
    load_v = pltpu.make_async_copy(values, full_v.at[:, pl.ds(off, own)], load_sem.at[0])
    load_l = pltpu.make_async_copy(lap_in, full_l.at[:, pl.ds(off, own)], load_sem.at[1])
    for w in range(walkers):
        pltpu.make_async_copy(tangent.at[w], tan.at[w], tan_sem.at[w]).start()
        if w == 0:
            load_v.start()
            load_l.start()

    barrier = pltpu.get_barrier_semaphore()
    pl.semaphore_signal(barrier, inc=1, device_id=partner, device_id_type=MESH)

    for k in range(1, XY):
        for other in (core, 1 - core):
            pl.semaphore_signal(
                barrier, inc=1, device_id=(across(k)[0], other), device_id_type=MESH
            )
    for k in range(1, NZ):
        pl.semaphore_signal(barrier, inc=1, device_id=(along(k), core), device_id_type=MESH)

    s8 = jnp.concatenate([slots[...]] * (8 // walkers), 0)
    r8 = iota((8, elec), 0) % walkers
    n8 = jnp.zeros((8, elec), jnp.int32)
    for w in range(walkers):
        n8 = jnp.where(r8 == w, spin[w], n8)
    upper = (s8 < n8).astype(F32).astype(BF16)
    spread = (iota((elec, rows), 0) == core * own + iota((elec, rows), 1) % own).astype(F32)
    tiled = dot(upper, spread.astype(BF16))
    eye = (iota((elec, elec), 0) == iota((elec, elec), 1)).astype(F32).astype(BF16)
    columns = lax.dot_general(eye, upper, (((1,), (1,)), ((), ())), preferred_element_type=F32)
    own_eye = (iota((own, elec), 0) + core * own == iota((own, elec), 1)).astype(F32).astype(BF16)
    own_columns = lax.dot_general(
        own_eye, upper, (((1,), (1,)), ((), ())), preferred_element_type=F32
    )
    r16 = iota((2 * BLOCK, rows), 0)
    c16 = iota((2 * BLOCK, rows), 1)
    for w in range(walkers):
        m = tiled[w : w + 1]
        m = jnp.where(r16 < BLOCK, m, 1.0 - m)
        sel[w] = jnp.where(c16 // own == r16 % BLOCK, m, 0.0).astype(BF16)

    def group_sums(w):
        pick = sel[w]

        def step(i, carry):
            d = pl.multiple_of(i * BLOCK, BLOCK)
            t = tan[w, pl.ds(d, BLOCK)].reshape(rows, feat)
            r = dot(pick, t)
            own_sums[w, 0, pl.ds(d, BLOCK)] = r[:BLOCK]
            own_sums[w, 1, pl.ds(d, BLOCK)] = r[BLOCK:]
            return carry

        lax.fori_loop(0, blocks, step, 0, unroll=4)

    def sums_copy(w):
        return pltpu.make_async_remote_copy(
            src_ref=own_sums.at[w],
            dst_ref=got_sums.at[w],
            send_sem=pair_send.at[w],
            recv_sem=pair_recv.at[w],
            device_id=partner,
            device_id_type=MESH,
        )

    def tan_wait(w):
        pltpu.make_async_copy(tangent.at[w], tan.at[w], tan_sem.at[w]).wait()

    ahead = 2
    tan_wait(0)
    group_sums(0)
    pl.semaphore_wait(barrier, 1 + 2 * (XY - 1) + NZ - 1)

    def to_partner(src, dst, i):
        return pltpu.make_async_remote_copy(
            src_ref=src,
            dst_ref=dst,
            send_sem=pair_send.at[i],
            recv_sem=pair_recv.at[i],
            device_id=partner,
            device_id_type=MESH,
        )

    send_v = to_partner(values, full_v.at[:, pl.ds(off, own)], walkers)
    send_l = to_partner(lap_in, full_l.at[:, pl.ds(off, own)], walkers + 1)
    send_v.start()
    send_l.start()
    sums_copy(0).start()
    for w in range(1, ahead):
        tan_wait(w)
        group_sums(w)
        sums_copy(w).start()
    load_v.wait()
    load_l.wait()
    send_v.wait()
    send_l.wait()

    gain = readout[...].reshape(1, feat)
    shift = bias[...].reshape(1, feat)
    row8 = iota((8, elec), 0)
    row81 = iota((8, 1), 0)
    total = jnp.zeros((feat, feat), F32)
    for w in range(walkers):
        n0 = spin[w].astype(F32)
        n1 = elec - n0
        up = upper[w : w + 1].astype(F32)
        masks = jnp.where(row8 == 0, up, jnp.where(row8 == 1, 1.0 - up, 0.0)).astype(BF16)
        counts = jnp.where(row81 == 0, n0, jnp.where(row81 == 1, n1, 1.0))
        mean_v = (dot(masks, full_v[w]) / counts).astype(BF16)
        mean_l = (dot(masks, full_l[w]) / counts).astype(BF16)
        mix_v = dot(mean_v, w_spin[...])
        mix_l = dot(mean_l, w_spin[...])
        is_up = columns[:, w : w + 1] > 0.5
        own_up = own_columns[:, w : w + 1] > 0.5
        pre = dot(full_v[w], w_self[...]) + jnp.where(is_up, mix_v[0:1], mix_v[1:2]) + shift
        squash = jnp.tanh(pre)
        slopes = 1.0 - squash * squash
        slopes_s[0, w] = slopes
        slopes_s[1, w] = -2.0 * squash * slopes
        lap_own = full_l[w, pl.ds(off, own)]
        lap_pre_s[w] = dot(lap_own, w_self[...]) + jnp.where(own_up, mix_l[0:1], mix_l[1:2])
        slope_bf = (slopes * gain).astype(BF16)
        mean_f = mean_v.astype(F32)
        picked = jnp.where(is_up, mean_f[0:1], mean_f[1:2])
        left = jnp.where(core == 0, full_v[w].astype(F32), picked).astype(BF16)
        term = lax.dot_general(
            left, slope_bf, (((0,), (0,)), ((), ())), preferred_element_type=F32
        )
        terms[w] = term.reshape(XY, 2, 8, feat)
        total = total + term
    shard_s[...] = total.reshape(shard_s.shape)

    def scatter(src, dst, i, whole=False):
        dst[here] = src[...] if whole else src[here]

        for k in range(1, XY):
            to, slot = across(k)
            pltpu.make_async_remote_copy(
                src_ref=src if whole else src.at[slot],
                dst_ref=dst.at[here],
                send_sem=rs_send.at[i, k],
                recv_sem=rs_recv.at[i, k],
                device_id=(to, core),
                device_id_type=MESH,
            ).start()

    def scatter_wait(src, dst, i, whole=False):
        for k in range(1, XY):
            to, slot = across(k)
            pltpu.make_async_remote_copy(
                src_ref=src if whole else src.at[slot],
                dst_ref=dst.at[behind(k)],
                send_sem=rs_send.at[i, k],
                recv_sem=rs_recv.at[i, k],
                device_id=(to, core),
                device_id_type=MESH,
            ).wait()

    def over_z(src, dst, i):
        dst[z] = src[...]
        for k in range(1, NZ):
            pltpu.make_async_remote_copy(
                src_ref=src,
                dst_ref=dst.at[z],
                send_sem=z_send.at[i, k],
                recv_sem=z_recv.at[i, k],
                device_id=(along(k), core),
                device_id_type=MESH,
            ).start()

    def over_z_wait(src, dst, i):
        for k in range(1, NZ):
            pltpu.make_async_remote_copy(
                src_ref=src,
                dst_ref=dst.at[lax.rem(z - k + NZ, NZ)],
                send_sem=z_send.at[i, k],
                recv_sem=z_recv.at[i, k],
                device_id=(along(k), core),
                device_id_type=MESH,
            ).wait()

    def add_up(ref, n):
        acc = ref[0]
        for j in range(1, n):
            acc = acc + ref[j]
        return acc

    scatter(shard_s, recv_s, 0)

    ones = jnp.ones((8, 128), F32)
    own_ex[...] = jnp.zeros((8, 256), F32)
    partial[dirs:] = jnp.zeros((256 - dirs, 128), F32)
    for w in range(walkers):
        if w + ahead < walkers:
            tan_wait(w + ahead)
            group_sums(w + ahead)
            sums_copy(w + ahead).start()
        sums_copy(w).wait()
        n0 = spin[w].astype(F32)
        inv = 1.0 / jnp.concatenate(
            [jnp.full((1, 1, 1), n0, F32), jnp.full((1, 1, 1), elec - n0, F32)], 0
        )
        means = ((own_sums[w] + got_sums[w]) * inv).astype(BF16)
        mixed[...] = dot(means.reshape(2 * dirs, feat), w_spin[...]).reshape(2, dirs, feat)
        own_up = jnp.broadcast_to(own_columns[:, w : w + 1], (own, feat)) > 0.5
        own_slopes = slopes_s[0, w, pl.ds(off, own)]
        own_curve = slopes_s[1, w, pl.ds(off, own)]
        weighted = own_slopes * gain

        def product(i, to):
            d = pl.multiple_of(i * STAGE, STAGE)
            t = tan[w, pl.ds(d, STAGE)].reshape(STAGE * own, feat)
            to[...] = dot(t, w_self[...])

        def use(i, a, part, acc):
            for j in range(STAGE):
                d = i * STAGE + j
                m0 = mixed[0, pl.ds(d, 1)]
                m1 = mixed[1, pl.ds(d, 1)]
                ch = a[j * own : (j + 1) * own] + jnp.where(own_up, m0, m1)
                acc = acc + ch * ch
                p = (ch * weighted).reshape(own // 8, 8, feat).sum(axis=0)
                part[8 * j : 8 * j + 8] = p[:, :128] + p[:, 128:]
            for b in range(STAGE // 8):
                r = part[pl.ds(64 * b, 8, stride=8)]
                for k in range(1, 8):
                    r = r + part[pl.ds(64 * b + k, 8, stride=8)]
                partial[pl.ds(pl.multiple_of(i * STAGE + b * 8, 8), 8)] = r
            return acc

        stages = dirs // STAGE

        def step(i, acc):
            product(2 * i + 1, prod_b)
            acc = use(2 * i, prod_a, part_a, acc)
            product(jnp.minimum(2 * i + 2, stages - 1), prod_a)
            return use(2 * i + 1, prod_b, part_b, acc)

        product(0, prod_a)
        squares = lax.fori_loop(0, stages // 2, step, jnp.zeros((own, feat), F32))
        lap = own_slopes * lap_pre_s[w] + own_curve * squares
        lap_out[w] = lap
        lp = (lap * gain).reshape(own // 8, 8, feat).sum(axis=0)
        partial[dirs : dirs + 1] = jnp.sum(lp[:, :128] + lp[:, 128:], axis=0, keepdims=True)
        g = lax.dot_general(
            ones, partial[...], (((1,), (1,)), ((), ())),
            precision=lax.Precision.HIGHEST, preferred_element_type=F32,
        )
        own_ex[...] = jnp.where(iota((8, 256), 0) == w, g, own_ex[...])
        if w == 2:
            scatter_wait(shard_s, recv_s, 0)
            mine_s[...] = add_up(recv_s, XY)
            over_z(mine_s, zs, 0)

    ex = to_partner(own_ex, got_ex, walkers + 2)
    ex.start()
    ex.wait()
    both = own_ex[...] + got_ex[...]
    lane = iota((8, 256), 1)
    both = jnp.where(lane < dirs, both * both, jnp.where(lane == dirs, both, 0.0))
    pot = jnp.zeros((8, 1), F32)
    for w in range(walkers):
        pot = jnp.where(row81 == w, potential[w], pot)
    energy = -0.5 * jnp.sum(both, axis=1, keepdims=True) + pot
    diagonal = iota((8, 128), 0) == iota((8, 128), 1)
    energy_out[...] = jnp.sum(jnp.where(diagonal, energy, 0.0), axis=0, keepdims=True)
    esum = jnp.sum(energy, axis=0, keepdims=True)
    own_e[...] = jnp.broadcast_to(esum, (1, 128))
    scatter(own_e, plane_e, 3, whole=True)
    for c in range(2):
        grad = energy[0:1] * terms[0, :, c]
        for w in range(1, walkers):
            grad = grad + energy[w : w + 1] * terms[w, :, c]
        shard_e[c] = grad
        scatter(shard_e.at[c], recv_e.at[c], 1 + c)
    over_z_wait(mine_s, zs, 0)
    scatter_wait(own_e, plane_e, 3, whole=True)
    mine_z[...] = add_up(plane_e, XY)
    over_z(mine_z, all_e, 3)
    local = mine_z[:, :1] / (walkers * XY)
    for c in range(2):
        scatter_wait(shard_e.at[c], recv_e.at[c], 1 + c)
        mine_e[c] = (add_up(recv_e.at[c], XY) - local * mine_s[c]).astype(BF16)
        over_z(mine_e.at[c], ze.at[c], 1 + c)
    over_z_wait(mine_z, all_e, 3)
    center = add_up(all_e, NZ)[:, :1] / (walkers * XY * NZ)
    rest = jnp.zeros((2, 8, feat), F32)
    for j in range(NZ):
        rest = rest + (all_e[j, :, :1] / (walkers * XY) - center) * zs[j]

    def gather_copy(k, other, matrix, slot, c, i):
        to, _ = across(k)
        return pltpu.make_async_remote_copy(
            src_ref=grads_out.at[core, c, here],
            dst_ref=grads_out.at[matrix, c, slot],
            send_sem=ag_send.at[2 * c + i, k],
            recv_sem=ag_recv.at[2 * c + i, k],
            device_id=(to, other),
            device_id_type=MESH,
        )

    for c in range(2):
        over_z_wait(mine_e.at[c], ze.at[c], 1 + c)
        grad = rest[c]
        for j in range(NZ):
            grad = grad + ze[c, j].astype(F32)
        grads_out[core, c, here] = grad.astype(BF16)
        gather_copy(0, 1 - core, core, here, c, 1).start()
        for k in range(1, XY):
            gather_copy(k, core, core, here, c, 0).start()
            gather_copy(k, 1 - core, core, here, c, 1).start()
    for c in range(2):
        gather_copy(0, 1 - core, 1 - core, here, c, 1).wait()
        for k in range(1, XY):
            gather_copy(k, core, core, behind(k), c, 0).wait()
            gather_copy(k, 1 - core, 1 - core, behind(k), c, 1).wait()


def results(lap, energy, grads, lap_out, energy_out, self_out, spin_out):
    lap_out[...] = lap[...]
    energy_out[...] = energy[0, : energy_out.shape[0]]
    for out, i in ((self_out, 0), (spin_out, 1)):
        halves = [grads[i, c].astype(F32)[:, None] for c in range(2)]
        out[...] = jnp.concatenate(halves, 1).reshape(out.shape)


def shards(
    values, lap_in, tangent, slot_electron, spin_up, w_self, w_spin, bias, readout, potential
):
    walkers, dirs, own, feat = tangent.shape
    elec = slot_electron.shape[1]
    per = feat // XY // 2
    vmem = pl.BlockSpec(memory_space=pltpu.VMEM)
    smem = pl.BlockSpec(memory_space=pltpu.SMEM)
    hbm = pl.BlockSpec(memory_space=pl.ANY)
    dma = pltpu.SemaphoreType.DMA
    lap, energy, grads = pl.pallas_call(
        body,
        out_shape=(
            jax.ShapeDtypeStruct((walkers, own, feat), F32),
            jax.ShapeDtypeStruct((1, 128), F32),
            jax.ShapeDtypeStruct((2, 2, XY, per, feat), BF16),
        ),
        in_specs=[hbm, hbm, hbm, vmem, smem, vmem, vmem, vmem, vmem, smem],
        out_specs=(vmem, vmem, vmem),
        scratch_shapes=[
            pltpu.VMEM((walkers, elec, feat), BF16),
            pltpu.VMEM((walkers, elec, feat), BF16),
            pltpu.VMEM((walkers, dirs, own, feat), BF16),
            pltpu.VMEM((walkers, 2, dirs, feat), F32),
            pltpu.VMEM((walkers, 2, dirs, feat), F32),
            pltpu.VMEM((2, dirs, feat), F32),
            pltpu.VMEM((walkers, 2 * BLOCK, BLOCK * own), BF16),
            pltpu.VMEM((walkers, XY, 2, per, feat), F32),
            pltpu.VMEM((2, walkers, elec, feat), F32),
            pltpu.VMEM((walkers, own, feat), F32),
            pltpu.VMEM((256, 128), F32),
            pltpu.VMEM((STAGE * own, feat), F32),
            pltpu.VMEM((STAGE * own, feat), F32),
            pltpu.VMEM((STAGE * 8, 128), F32),
            pltpu.VMEM((STAGE * 8, 128), F32),
            pltpu.VMEM((8, 256), F32),
            pltpu.VMEM((8, 256), F32),
            pltpu.VMEM((XY, 2, per, feat), F32),
            pltpu.VMEM((XY, 2, per, feat), F32),
            pltpu.VMEM((2, per, feat), F32),
            pltpu.VMEM((NZ, 2, per, feat), F32),
            pltpu.VMEM((2, XY, per, feat), F32),
            pltpu.VMEM((2, XY, per, feat), F32),
            pltpu.VMEM((2, per, feat), BF16),
            pltpu.VMEM((2, NZ, per, feat), BF16),
            pltpu.VMEM((1, 128), F32),
            pltpu.VMEM((XY, 1, 128), F32),
            pltpu.VMEM((1, 128), F32),
            pltpu.VMEM((NZ, 1, 128), F32),
            dma((2,)),
            dma((walkers,)),
            dma((walkers + 3,)),
            dma((walkers + 3,)),
            dma((4, XY)),
            dma((4, XY)),
            dma((4, NZ)),
            dma((4, NZ)),
            dma((4, XY)),
            dma((4, XY)),
        ],
        compiler_params=pltpu.CompilerParams(
            collective_id=0, has_side_effects=True, vmem_limit_bytes=60 << 20
        ),
        name="forward_laplacian",
    )(values, lap_in, tangent, slot_electron, spin_up, w_self, w_spin, bias, readout, potential)
    return pl.pallas_call(
        results,
        out_shape=(
            jax.ShapeDtypeStruct((walkers, own, feat), F32),
            jax.ShapeDtypeStruct((walkers,), F32),
            jax.ShapeDtypeStruct((feat, feat), F32),
            jax.ShapeDtypeStruct((feat, feat), F32),
        ),
        in_specs=[vmem, vmem, vmem],
        out_specs=(vmem, vmem, vmem, vmem),
        name="results",
    )(lap, energy, grads)


def solution(mesh):
    placed = (
        P("walk", "tan", None),
        P("walk", "tan", None),
        P("walk", None, "tan", None),
        P("walk", None),
        P("walk"),
        P(),
        P(),
        P(),
        P(),
        P("walk"),
    )
    return jax.shard_map(
        shards,
        mesh=mesh,
        in_specs=placed,
        out_specs=(P("walk", "tan", None), P("walk"), P(), P()),
        check_vma=False,
    )
```

```python
import jax
import jax.numpy as jnp
from jax import lax
from jax.experimental import pallas as pl
from jax.experimental.pallas import tpu as pltpu
from jax.sharding import PartitionSpec as P

MESH = pl.DeviceIdType.MESH
F32 = jnp.float32
BF16 = jnp.bfloat16
NX, NZ, NY = 4, 8, 4
XY = NX * NY
FAR_XY = (10, 6, 9, 11, 14, 2, 8, 5, 7, 13, 15, 1, 3, 4, 12)
FAR_Z = (4, 3, 5, 2, 6, 1, 7)
BLOCK = 8
STAGE = 32


def iota(shape, axis):
    return lax.broadcasted_iota(jnp.int32, shape, axis)


def dot(a, b):
    return jnp.dot(a, b, preferred_element_type=F32)


def body(
    values, lap_in, tangent, slots_in, spin, w_self_in, w_spin_in, bias_in, readout_in, potential,
    lap_out, energy_out, grads_out,
    full_v, full_l, tan, own_sums, got_sums, mixed, sel, terms, slopes_s, lap_pre_s,
    partial, prod_a, prod_b, part_a, part_b, own_ex, got_ex, shard_s, recv_s, mine_s, zs, shard_e, recv_e, mine_e, ze,
    own_e, plane_e, mine_z, all_e,
    slots, w_self, w_spin, bias, readout,
    load_sem, tan_sem, pair_send, pair_recv,
    rs_send, rs_recv, z_send, z_recv, ag_send, ag_recv,
):
    walkers, dirs, own, feat = tangent.shape
    elec = slots_in.shape[1]
    rows = BLOCK * own
    blocks = dirs // BLOCK
    me = lax.axis_index("walk")
    core = lax.axis_index("tan")
    x = lax.div(me, NZ * NY)
    z = lax.rem(lax.div(me, NY), NZ)
    y = lax.rem(me, NY)
    here = x * NY + y
    partner = (me, 1 - core)
    xs = [x] + [lax.rem(x + i, NX) for i in range(1, NX)]
    ys = [y] + [lax.rem(y + i, NY) for i in range(1, NY)]
    lines = [xs[i] * (NZ * NY) + z * NY for i in range(NX)]
    columns_z = [me] + [x * (NZ * NY) + lax.rem(z + i, NZ) * NY + y for i in range(1, NZ)]

    def across(k):
        return lines[k // NY] + ys[k % NY], xs[k // NY] * NY + ys[k % NY]

    def behind(k):
        return xs[-(k // NY) % NX] * NY + ys[-(k % NY) % NY]

    def along(k):
        return columns_z[k]

    off = pl.multiple_of(core * own, own)
    load_v = pltpu.make_async_copy(values, full_v.at[:, pl.ds(off, own)], load_sem.at[0])
    load_l = pltpu.make_async_copy(lap_in, full_l.at[:, pl.ds(off, own)], load_sem.at[1])
    small = [
        pltpu.make_async_copy(src, dst, load_sem.at[2 + i])
        for i, (src, dst) in enumerate(
            (
                (slots_in, slots),
                (w_self_in, w_self),
                (w_spin_in, w_spin),
                (bias_in, bias),
                (readout_in, readout),
            )
        )
    ]
    small[0].start()
    for w in range(walkers):
        pltpu.make_async_copy(tangent.at[w], tan.at[w], tan_sem.at[w]).start()
        if w == 0:
            load_v.start()
            load_l.start()
            for copy in small[1:]:
                copy.start()

    barrier = pltpu.get_barrier_semaphore()
    pl.semaphore_signal(barrier, inc=1, device_id=partner, device_id_type=MESH)

    for k in range(1, XY):
        pl.semaphore_signal(barrier, inc=1, device_id=(across(k)[0], core), device_id_type=MESH)
    for k in range(1, NZ):
        pl.semaphore_signal(barrier, inc=1, device_id=(along(k), core), device_id_type=MESH)

    small[0].wait()
    s8 = jnp.concatenate([slots[...]] * (8 // walkers), 0)
    r8 = iota((8, elec), 0) % walkers
    n8 = jnp.zeros((8, elec), jnp.int32)
    for w in range(walkers):
        n8 = jnp.where(r8 == w, spin[w], n8)
    upper = (s8 < n8).astype(F32).astype(BF16)
    spread = (iota((elec, rows), 0) == core * own + iota((elec, rows), 1) % own).astype(F32)
    tiled = dot(upper, spread.astype(BF16))
    eye = (iota((elec, elec), 0) == iota((elec, elec), 1)).astype(F32).astype(BF16)
    columns = lax.dot_general(eye, upper, (((1,), (1,)), ((), ())), preferred_element_type=F32)
    own_eye = (iota((own, elec), 0) + core * own == iota((own, elec), 1)).astype(F32).astype(BF16)
    own_columns = lax.dot_general(
        own_eye, upper, (((1,), (1,)), ((), ())), preferred_element_type=F32
    )
    r16 = iota((2 * BLOCK, rows), 0)
    c16 = iota((2 * BLOCK, rows), 1)
    for w in range(walkers):
        m = tiled[w : w + 1]
        m = jnp.where(r16 < BLOCK, m, 1.0 - m)
        sel[w] = jnp.where(c16 // own == r16 % BLOCK, m, 0.0).astype(BF16)

    def group_sums(w):
        pick = sel[w]

        def step(i, carry):
            d = pl.multiple_of(i * BLOCK, BLOCK)
            t = tan[w, pl.ds(d, BLOCK)].reshape(rows, feat)
            r = dot(pick, t)
            own_sums[w, 0, pl.ds(d, BLOCK)] = r[:BLOCK]
            own_sums[w, 1, pl.ds(d, BLOCK)] = r[BLOCK:]
            return carry

        lax.fori_loop(0, blocks, step, 0, unroll=4)

    def sums_copy(w):
        return pltpu.make_async_remote_copy(
            src_ref=own_sums.at[w],
            dst_ref=got_sums.at[w],
            send_sem=pair_send.at[w],
            recv_sem=pair_recv.at[w],
            device_id=partner,
            device_id_type=MESH,
        )

    def tan_wait(w):
        pltpu.make_async_copy(tangent.at[w], tan.at[w], tan_sem.at[w]).wait()

    ahead = 3
    for w in range(2):
        tan_wait(w)
        group_sums(w)
    pl.semaphore_wait(barrier, 1 + (XY - 1) + NZ - 1)

    def to_partner(src, dst, i):
        return pltpu.make_async_remote_copy(
            src_ref=src,
            dst_ref=dst,
            send_sem=pair_send.at[i],
            recv_sem=pair_recv.at[i],
            device_id=partner,
            device_id_type=MESH,
        )

    send_v = to_partner(values, full_v.at[:, pl.ds(off, own)], walkers)
    send_l = to_partner(lap_in, full_l.at[:, pl.ds(off, own)], walkers + 1)
    send_v.start()
    send_l.start()
    sums_copy(0).start()
    sums_copy(1).start()
    for w in range(2, ahead):
        tan_wait(w)
        group_sums(w)
        sums_copy(w).start()
    for copy in small[1:]:
        copy.wait()
    load_v.wait()
    load_l.wait()
    send_v.wait()
    send_l.wait()

    gain = readout[...].reshape(1, feat)
    shift = bias[...].reshape(1, feat)
    row8 = iota((8, elec), 0)
    row81 = iota((8, 1), 0)
    total = jnp.zeros((feat, feat), F32)
    for w in range(walkers):
        n0 = spin[w].astype(F32)
        n1 = elec - n0
        up = upper[w : w + 1].astype(F32)
        masks = jnp.where(row8 == 0, up, jnp.where(row8 == 1, 1.0 - up, 0.0)).astype(BF16)
        counts = jnp.where(row81 == 0, n0, jnp.where(row81 == 1, n1, 1.0))
        mean_v = (dot(masks, full_v[w]) / counts).astype(BF16)
        mean_l = (dot(masks, full_l[w]) / counts).astype(BF16)
        mix_v = dot(mean_v, w_spin[...])
        mix_l = dot(mean_l, w_spin[...])
        is_up = columns[:, w : w + 1] > 0.5
        own_up = own_columns[:, w : w + 1] > 0.5
        pre = dot(full_v[w], w_self[...]) + jnp.where(is_up, mix_v[0:1], mix_v[1:2]) + shift
        squash = jnp.tanh(pre)
        slopes = 1.0 - squash * squash
        slopes_s[0, w] = slopes
        slopes_s[1, w] = -2.0 * squash * slopes
        lap_own = full_l[w, pl.ds(off, own)]
        lap_pre_s[w] = dot(lap_own, w_self[...]) + jnp.where(own_up, mix_l[0:1], mix_l[1:2])
        slope_bf = (slopes * gain).astype(BF16)
        mean_f = mean_v.astype(F32)
        picked = jnp.where(is_up, mean_f[0:1], mean_f[1:2])
        left = jnp.where(core == 0, full_v[w].astype(F32), picked).astype(BF16)
        term = lax.dot_general(
            left, slope_bf, (((0,), (0,)), ((), ())), preferred_element_type=F32
        )
        terms[w] = term.reshape(XY, 2, 8, feat)
        total = total + term
    shard_s[...] = total.reshape(shard_s.shape)

    def scatter(src, dst, i, whole=False):
        dst[here] = src[...] if whole else src[here]

        for k in FAR_XY:
            to, slot = across(k)
            pltpu.make_async_remote_copy(
                src_ref=src if whole else src.at[slot],
                dst_ref=dst.at[here],
                send_sem=rs_send.at[i, k],
                recv_sem=rs_recv.at[i, k],
                device_id=(to, core),
                device_id_type=MESH,
            ).start()

    def scatter_wait(src, dst, i, whole=False):
        for k in FAR_XY:
            to, slot = across(k)
            pltpu.make_async_remote_copy(
                src_ref=src if whole else src.at[slot],
                dst_ref=dst.at[behind(k)],
                send_sem=rs_send.at[i, k],
                recv_sem=rs_recv.at[i, k],
                device_id=(to, core),
                device_id_type=MESH,
            ).wait()

    def over_z(src, dst, i):
        dst[z] = src[...]
        for k in FAR_Z:
            pltpu.make_async_remote_copy(
                src_ref=src,
                dst_ref=dst.at[z],
                send_sem=z_send.at[i, k],
                recv_sem=z_recv.at[i, k],
                device_id=(along(k), core),
                device_id_type=MESH,
            ).start()

    def over_z_wait(src, dst, i):
        for k in FAR_Z:
            pltpu.make_async_remote_copy(
                src_ref=src,
                dst_ref=dst.at[lax.rem(z - k + NZ, NZ)],
                send_sem=z_send.at[i, k],
                recv_sem=z_recv.at[i, k],
                device_id=(along(k), core),
                device_id_type=MESH,
            ).wait()

    def add_up(ref, n):
        acc = ref[0]
        for j in range(1, n):
            acc = acc + ref[j]
        return acc

    scatter(shard_s, recv_s, 0)

    ones = jnp.ones((8, 128), F32)
    own_ex[...] = jnp.zeros((8, 256), F32)
    partial[dirs:] = jnp.zeros((256 - dirs, 128), F32)
    for w in range(walkers):
        if w + ahead < walkers:
            tan_wait(w + ahead)
            group_sums(w + ahead)
            sums_copy(w + ahead).start()
        sums_copy(w).wait()
        n0 = spin[w].astype(F32)
        inv = 1.0 / jnp.concatenate(
            [jnp.full((1, 1, 1), n0, F32), jnp.full((1, 1, 1), elec - n0, F32)], 0
        )
        means = ((own_sums[w] + got_sums[w]) * inv).astype(BF16)
        mixed[...] = dot(means.reshape(2 * dirs, feat), w_spin[...]).reshape(2, dirs, feat)
        own_up = jnp.broadcast_to(own_columns[:, w : w + 1], (own, feat)) > 0.5
        own_slopes = slopes_s[0, w, pl.ds(off, own)]
        own_curve = slopes_s[1, w, pl.ds(off, own)]
        weighted = own_slopes * gain

        def product(i, to):
            d = pl.multiple_of(i * STAGE, STAGE)
            t = tan[w, pl.ds(d, STAGE)].reshape(STAGE * own, feat)
            to[...] = dot(t, w_self[...])

        def use(i, a, part, acc):
            for j in range(STAGE):
                d = i * STAGE + j
                m0 = mixed[0, pl.ds(d, 1)]
                m1 = mixed[1, pl.ds(d, 1)]
                ch = a[j * own : (j + 1) * own] + jnp.where(own_up, m0, m1)
                acc = acc + ch * ch
                p = (ch * weighted).reshape(own // 8, 8, feat).sum(axis=0)
                part[8 * j : 8 * j + 8] = p[:, :128] + p[:, 128:]
            for b in range(STAGE // 8):
                r = part[pl.ds(64 * b, 8, stride=8)]
                for k in range(1, 8):
                    r = r + part[pl.ds(64 * b + k, 8, stride=8)]
                partial[pl.ds(pl.multiple_of(i * STAGE + b * 8, 8), 8)] = r
            return acc

        stages = dirs // STAGE

        def step(i, acc):
            product(2 * i + 1, prod_b)
            acc = use(2 * i, prod_a, part_a, acc)
            product(jnp.minimum(2 * i + 2, stages - 1), prod_a)
            return use(2 * i + 1, prod_b, part_b, acc)

        product(0, prod_a)
        squares = lax.fori_loop(0, stages // 2, step, jnp.zeros((own, feat), F32))
        lap = own_slopes * lap_pre_s[w] + own_curve * squares
        lap_out[w] = lap
        lp = (lap * gain).reshape(own // 8, 8, feat).sum(axis=0)
        partial[dirs : dirs + 1] = jnp.sum(lp[:, :128] + lp[:, 128:], axis=0, keepdims=True)
        g = lax.dot_general(
            ones, partial[...], (((1,), (1,)), ((), ())),
            precision=lax.Precision.HIGHEST, preferred_element_type=F32,
        )
        own_ex[...] = jnp.where(iota((8, 256), 0) == w, g, own_ex[...])
    ex = to_partner(own_ex, got_ex, walkers + 2)
    ex.start()
    scatter_wait(shard_s, recv_s, 0)
    mine_s[...] = add_up(recv_s, XY)
    over_z(mine_s, zs, 0)
    ex.wait()
    both = own_ex[...] + got_ex[...]
    lane = iota((8, 256), 1)
    both = jnp.where(lane < dirs, both * both, jnp.where(lane == dirs, both, 0.0))
    pot = jnp.zeros((8, 1), F32)
    for w in range(walkers):
        pot = jnp.where(row81 == w, potential[w], pot)
    energy = -0.5 * jnp.sum(both, axis=1, keepdims=True) + pot
    diagonal = iota((8, 128), 0) == iota((8, 128), 1)
    energy_out[...] = jnp.sum(jnp.where(diagonal, energy, 0.0), axis=0, keepdims=True)
    esum = jnp.sum(energy, axis=0, keepdims=True)
    own_e[...] = jnp.broadcast_to(esum, (1, 128))
    scatter(own_e, plane_e, 3, whole=True)
    for c in range(2):
        grad = energy[0:1] * terms[0, :, c]
        for w in range(1, walkers):
            grad = grad + energy[w : w + 1] * terms[w, :, c]
        shard_e[c] = grad
        scatter(shard_e.at[c], recv_e.at[c], 1 + c)
    scatter_wait(own_e, plane_e, 3, whole=True)
    mine_z[...] = add_up(plane_e, XY)
    over_z(mine_z, all_e, 3)
    local = mine_z[:, :1] / (walkers * XY)
    for c in range(2):
        scatter_wait(shard_e.at[c], recv_e.at[c], 1 + c)
        mine_e[c] = (add_up(recv_e.at[c], XY) - local * mine_s[c]).astype(BF16)
        over_z(mine_e.at[c], ze.at[c], 1 + c)
    over_z_wait(mine_s, zs, 0)
    over_z_wait(mine_z, all_e, 3)
    center = add_up(all_e, NZ)[:, :1] / (walkers * XY * NZ)
    rest = jnp.zeros((2, 8, feat), F32)
    for j in range(NZ):
        rest = rest + (all_e[j, :, :1] / (walkers * XY) - center) * zs[j]

    def gather_copy(k, slot, c):
        return pltpu.make_async_remote_copy(
            src_ref=grads_out.at[core, c, here],
            dst_ref=grads_out.at[core, c, slot],
            send_sem=ag_send.at[c, k],
            recv_sem=ag_recv.at[c, k],
            device_id=(across(k)[0], core),
            device_id_type=MESH,
        )

    def hand_over(matrix, c):
        return pltpu.make_async_remote_copy(
            src_ref=grads_out.at[core, c],
            dst_ref=grads_out.at[matrix, c],
            send_sem=ag_send.at[c, 0],
            recv_sem=ag_recv.at[c, 0],
            device_id=partner,
            device_id_type=MESH,
        )

    for c in range(2):
        over_z_wait(mine_e.at[c], ze.at[c], 1 + c)
        grad = rest[c]
        for j in range(NZ):
            grad = grad + ze[c, j].astype(F32)
        grads_out[core, c, here] = grad.astype(BF16)
        for k in FAR_XY:
            gather_copy(k, here, c).start()
    for c in range(2):
        for k in FAR_XY:
            gather_copy(k, behind(k), c).wait()
        hand_over(core, c).start()
    for c in range(2):
        hand_over(1 - core, c).wait()


def results(lap, energy, grads, lap_out, energy_out, self_out, spin_out):
    lap_out[...] = lap[...]
    energy_out[...] = energy[0, : energy_out.shape[0]]
    for out, i in ((self_out, 0), (spin_out, 1)):
        halves = [grads[i, c].astype(F32)[:, None] for c in range(2)]
        out[...] = jnp.concatenate(halves, 1).reshape(out.shape)


def shards(
    values, lap_in, tangent, slot_electron, spin_up, w_self, w_spin, bias, readout, potential
):
    walkers, dirs, own, feat = tangent.shape
    elec = slot_electron.shape[1]
    per = feat // XY // 2
    vmem = pl.BlockSpec(memory_space=pltpu.VMEM)
    smem = pl.BlockSpec(memory_space=pltpu.SMEM)
    hbm = pl.BlockSpec(memory_space=pl.ANY)
    dma = pltpu.SemaphoreType.DMA
    lap, energy, grads = pl.pallas_call(
        body,
        out_shape=(
            jax.ShapeDtypeStruct((walkers, own, feat), F32),
            jax.ShapeDtypeStruct((1, 128), F32),
            jax.ShapeDtypeStruct((2, 2, XY, per, feat), BF16),
        ),
        in_specs=[hbm, hbm, hbm, hbm, smem, hbm, hbm, hbm, hbm, smem],
        out_specs=(vmem, vmem, vmem),
        scratch_shapes=[
            pltpu.VMEM((walkers, elec, feat), BF16),
            pltpu.VMEM((walkers, elec, feat), BF16),
            pltpu.VMEM((walkers, dirs, own, feat), BF16),
            pltpu.VMEM((walkers, 2, dirs, feat), F32),
            pltpu.VMEM((walkers, 2, dirs, feat), F32),
            pltpu.VMEM((2, dirs, feat), F32),
            pltpu.VMEM((walkers, 2 * BLOCK, BLOCK * own), BF16),
            pltpu.VMEM((walkers, XY, 2, per, feat), F32),
            pltpu.VMEM((2, walkers, elec, feat), F32),
            pltpu.VMEM((walkers, own, feat), F32),
            pltpu.VMEM((256, 128), F32),
            pltpu.VMEM((STAGE * own, feat), F32),
            pltpu.VMEM((STAGE * own, feat), F32),
            pltpu.VMEM((STAGE * 8, 128), F32),
            pltpu.VMEM((STAGE * 8, 128), F32),
            pltpu.VMEM((8, 256), F32),
            pltpu.VMEM((8, 256), F32),
            pltpu.VMEM((XY, 2, per, feat), F32),
            pltpu.VMEM((XY, 2, per, feat), F32),
            pltpu.VMEM((2, per, feat), F32),
            pltpu.VMEM((NZ, 2, per, feat), F32),
            pltpu.VMEM((2, XY, per, feat), F32),
            pltpu.VMEM((2, XY, per, feat), F32),
            pltpu.VMEM((2, per, feat), BF16),
            pltpu.VMEM((2, NZ, per, feat), BF16),
            pltpu.VMEM((1, 128), F32),
            pltpu.VMEM((XY, 1, 128), F32),
            pltpu.VMEM((1, 128), F32),
            pltpu.VMEM((NZ, 1, 128), F32),
            pltpu.VMEM((walkers, elec), jnp.int32),
            pltpu.VMEM((feat, feat), BF16),
            pltpu.VMEM((feat, feat), BF16),
            pltpu.VMEM((feat,), F32),
            pltpu.VMEM((feat,), F32),
            dma((7,)),
            dma((walkers,)),
            dma((walkers + 3,)),
            dma((walkers + 3,)),
            dma((4, XY)),
            dma((4, XY)),
            dma((4, NZ)),
            dma((4, NZ)),
            dma((2, XY)),
            dma((2, XY)),
        ],
        compiler_params=pltpu.CompilerParams(
            collective_id=0, has_side_effects=True, vmem_limit_bytes=60 << 20
        ),
        name="forward_laplacian",
    )(values, lap_in, tangent, slot_electron, spin_up, w_self, w_spin, bias, readout, potential)
    return pl.pallas_call(
        results,
        out_shape=(
            jax.ShapeDtypeStruct((walkers, own, feat), F32),
            jax.ShapeDtypeStruct((walkers,), F32),
            jax.ShapeDtypeStruct((feat, feat), F32),
            jax.ShapeDtypeStruct((feat, feat), F32),
        ),
        in_specs=[vmem, vmem, vmem],
        out_specs=(vmem, vmem, vmem, vmem),
        name="results",
    )(lap, energy, grads)


def solution(mesh):
    placed = (
        P("walk", "tan", None),
        P("walk", "tan", None),
        P("walk", None, "tan", None),
        P("walk", None),
        P("walk"),
        P(),
        P(),
        P(),
        P(),
        P("walk"),
    )
    return jax.shard_map(
        shards,
        mesh=mesh,
        in_specs=placed,
        out_specs=(P("walk", "tan", None), P("walk"), P(), P()),
        check_vma=False,
    )
```

```python
import jax
import jax.numpy as jnp
from jax import lax
from jax.experimental import pallas as pl
from jax.experimental.pallas import tpu as pltpu
from jax.sharding import PartitionSpec as P

MESH = pl.DeviceIdType.MESH
F32 = jnp.float32
BF16 = jnp.bfloat16
NX, NZ, NY = 4, 8, 4
XY = NX * NY
FAR_XY = (10, 6, 9, 11, 14, 2, 8, 5, 7, 13, 15, 1, 3, 4, 12)
FAR_Z = (4, 3, 5, 2, 6, 1, 7)
BLOCK = 8
STAGE = 32


def iota(shape, axis):
    return lax.broadcasted_iota(jnp.int32, shape, axis)


def dot(a, b):
    return jnp.dot(a, b, preferred_element_type=F32)


def body(
    values, lap_in, tangent, slots_in, spin, w_self_in, w_spin_in, bias_in, readout_in, potential,
    lap_out, energy_out, grads_out,
    full_v, full_l, tan, own_sums, got_sums, mixed, sel, terms, slopes_s, lap_pre_s,
    partial, prod_a, prod_b, part_a, part_b, own_ex, got_ex, shard_s, recv_s, mine_s, zs, shard_e, recv_e, mine_e, ze,
    own_e, plane_e, mine_z, all_e,
    slots, w_self, w_spin, bias, readout,
    load_sem, tan_sem, pair_send, pair_recv,
    rs_send, rs_recv, z_send, z_recv, ag_send, ag_recv,
):
    walkers, dirs, own, feat = tangent.shape
    elec = slots_in.shape[1]
    rows = BLOCK * own
    blocks = dirs // BLOCK
    me = lax.axis_index("walk")
    core = lax.axis_index("tan")
    x = lax.div(me, NZ * NY)
    z = lax.rem(lax.div(me, NY), NZ)
    y = lax.rem(me, NY)
    here = x * NY + y
    partner = (me, 1 - core)
    xs = [x] + [lax.rem(x + i, NX) for i in range(1, NX)]
    ys = [y] + [lax.rem(y + i, NY) for i in range(1, NY)]
    lines = [xs[i] * (NZ * NY) + z * NY for i in range(NX)]
    columns_z = [me] + [x * (NZ * NY) + lax.rem(z + i, NZ) * NY + y for i in range(1, NZ)]

    def across(k):
        return lines[k // NY] + ys[k % NY], xs[k // NY] * NY + ys[k % NY]

    def behind(k):
        return xs[-(k // NY) % NX] * NY + ys[-(k % NY) % NY]

    def along(k):
        return columns_z[k]

    off = pl.multiple_of(core * own, own)
    load_v = pltpu.make_async_copy(values, full_v.at[:, pl.ds(off, own)], load_sem.at[0])
    load_l = pltpu.make_async_copy(lap_in, full_l.at[:, pl.ds(off, own)], load_sem.at[1])
    small = [
        pltpu.make_async_copy(src, dst, load_sem.at[2 + i])
        for i, (src, dst) in enumerate(
            (
                (slots_in, slots),
                (w_self_in, w_self),
                (w_spin_in, w_spin),
                (bias_in, bias),
                (readout_in, readout),
            )
        )
    ]
    small[0].start()
    for w in range(walkers):
        pltpu.make_async_copy(tangent.at[w], tan.at[w], tan_sem.at[w]).start()
        if w == 0:
            load_v.start()
            load_l.start()
            for copy in small[1:]:
                copy.start()

    barrier = pltpu.get_barrier_semaphore()
    pl.semaphore_signal(barrier, inc=1, device_id=partner, device_id_type=MESH)

    for k in range(1, XY):
        pl.semaphore_signal(barrier, inc=1, device_id=(across(k)[0], core), device_id_type=MESH)
    for k in range(1, NZ):
        pl.semaphore_signal(barrier, inc=1, device_id=(along(k), core), device_id_type=MESH)

    small[0].wait()
    s8 = jnp.concatenate([slots[...]] * (8 // walkers), 0)
    r8 = iota((8, elec), 0) % walkers
    n8 = jnp.zeros((8, elec), jnp.int32)
    for w in range(walkers):
        n8 = jnp.where(r8 == w, spin[w], n8)
    upper = (s8 < n8).astype(F32).astype(BF16)
    spread = (iota((elec, rows), 0) == core * own + iota((elec, rows), 1) % own).astype(F32)
    tiled = dot(upper, spread.astype(BF16))
    eye = (iota((elec, elec), 0) == iota((elec, elec), 1)).astype(F32).astype(BF16)
    columns = lax.dot_general(eye, upper, (((1,), (1,)), ((), ())), preferred_element_type=F32)
    own_eye = (iota((own, elec), 0) + core * own == iota((own, elec), 1)).astype(F32).astype(BF16)
    own_columns = lax.dot_general(
        own_eye, upper, (((1,), (1,)), ((), ())), preferred_element_type=F32
    )
    r16 = iota((2 * BLOCK, rows), 0)
    c16 = iota((2 * BLOCK, rows), 1)
    for w in range(walkers):
        m = tiled[w : w + 1]
        m = jnp.where(r16 < BLOCK, m, 1.0 - m)
        sel[w] = jnp.where(c16 // own == r16 % BLOCK, m, 0.0).astype(BF16)

    def group_sums(w):
        pick = sel[w]

        def step(i, carry):
            d = pl.multiple_of(i * BLOCK, BLOCK)
            t = tan[w, pl.ds(d, BLOCK)].reshape(rows, feat)
            r = dot(pick, t)
            own_sums[w, 0, pl.ds(d, BLOCK)] = r[:BLOCK]
            own_sums[w, 1, pl.ds(d, BLOCK)] = r[BLOCK:]
            return carry

        lax.fori_loop(0, blocks, step, 0, unroll=4)

    def sums_copy(w):
        return pltpu.make_async_remote_copy(
            src_ref=own_sums.at[w],
            dst_ref=got_sums.at[w],
            send_sem=pair_send.at[w],
            recv_sem=pair_recv.at[w],
            device_id=partner,
            device_id_type=MESH,
        )

    def tan_wait(w):
        pltpu.make_async_copy(tangent.at[w], tan.at[w], tan_sem.at[w]).wait()

    ahead = 3
    for w in range(2):
        tan_wait(w)
        group_sums(w)
    pl.semaphore_wait(barrier, 1 + (XY - 1) + NZ - 1)

    def to_partner(src, dst, i):
        return pltpu.make_async_remote_copy(
            src_ref=src,
            dst_ref=dst,
            send_sem=pair_send.at[i],
            recv_sem=pair_recv.at[i],
            device_id=partner,
            device_id_type=MESH,
        )

    send_v = to_partner(values, full_v.at[:, pl.ds(off, own)], walkers)
    send_l = to_partner(lap_in, full_l.at[:, pl.ds(off, own)], walkers + 1)
    send_v.start()
    send_l.start()
    sums_copy(0).start()
    sums_copy(1).start()
    for w in range(2, ahead):
        tan_wait(w)
        group_sums(w)
        sums_copy(w).start()
    for copy in small[1:]:
        copy.wait()
    load_v.wait()
    load_l.wait()
    send_v.wait()
    send_l.wait()

    gain = readout[...].reshape(1, feat)
    shift = bias[...].reshape(1, feat)
    row8 = iota((8, elec), 0)
    row81 = iota((8, 1), 0)
    total = jnp.zeros((feat, feat), F32)
    for w in range(walkers):
        n0 = spin[w].astype(F32)
        n1 = elec - n0
        up = upper[w : w + 1].astype(F32)
        masks = jnp.where(row8 == 0, up, jnp.where(row8 == 1, 1.0 - up, 0.0)).astype(BF16)
        counts = jnp.where(row81 == 0, n0, jnp.where(row81 == 1, n1, 1.0))
        mean_v = (dot(masks, full_v[w]) / counts).astype(BF16)
        mean_l = (dot(masks, full_l[w]) / counts).astype(BF16)
        mix_v = dot(mean_v, w_spin[...])
        mix_l = dot(mean_l, w_spin[...])
        is_up = columns[:, w : w + 1] > 0.5
        own_up = own_columns[:, w : w + 1] > 0.5
        pre = dot(full_v[w], w_self[...]) + jnp.where(is_up, mix_v[0:1], mix_v[1:2]) + shift
        squash = jnp.tanh(pre)
        slopes = 1.0 - squash * squash
        slopes_s[0, w] = slopes
        slopes_s[1, w] = -2.0 * squash * slopes
        lap_own = full_l[w, pl.ds(off, own)]
        lap_pre_s[w] = dot(lap_own, w_self[...]) + jnp.where(own_up, mix_l[0:1], mix_l[1:2])
        slope_bf = (slopes * gain).astype(BF16)
        mean_f = mean_v.astype(F32)
        picked = jnp.where(is_up, mean_f[0:1], mean_f[1:2])
        left = jnp.where(core == 0, full_v[w].astype(F32), picked).astype(BF16)
        term = lax.dot_general(
            left, slope_bf, (((0,), (0,)), ((), ())), preferred_element_type=F32
        )
        terms[w] = term.reshape(XY, 2, 8, feat)
        total = total + term
    shard_s[...] = total.reshape(shard_s.shape)

    def scatter(src, dst, i, whole=False):
        dst[here] = src[...] if whole else src[here]

        for k in FAR_XY:
            to, slot = across(k)
            pltpu.make_async_remote_copy(
                src_ref=src if whole else src.at[slot],
                dst_ref=dst.at[here],
                send_sem=rs_send.at[i, k],
                recv_sem=rs_recv.at[i, k],
                device_id=(to, core),
                device_id_type=MESH,
            ).start()

    def scatter_wait(src, dst, i, whole=False):
        for k in FAR_XY:
            to, slot = across(k)
            pltpu.make_async_remote_copy(
                src_ref=src if whole else src.at[slot],
                dst_ref=dst.at[behind(k)],
                send_sem=rs_send.at[i, k],
                recv_sem=rs_recv.at[i, k],
                device_id=(to, core),
                device_id_type=MESH,
            ).wait()

    def over_z(src, dst, i):
        dst[z] = src[...]
        for k in FAR_Z:
            pltpu.make_async_remote_copy(
                src_ref=src,
                dst_ref=dst.at[z],
                send_sem=z_send.at[i, k],
                recv_sem=z_recv.at[i, k],
                device_id=(along(k), core),
                device_id_type=MESH,
            ).start()

    def over_z_wait(src, dst, i):
        for k in FAR_Z:
            pltpu.make_async_remote_copy(
                src_ref=src,
                dst_ref=dst.at[lax.rem(z - k + NZ, NZ)],
                send_sem=z_send.at[i, k],
                recv_sem=z_recv.at[i, k],
                device_id=(along(k), core),
                device_id_type=MESH,
            ).wait()

    def add_up(ref, n):
        acc = ref[0]
        for j in range(1, n):
            acc = acc + ref[j]
        return acc

    scatter(shard_s, recv_s, 0)

    ones = jnp.ones((8, 128), F32)
    own_ex[...] = jnp.zeros((8, 256), F32)
    partial[dirs:] = jnp.zeros((256 - dirs, 128), F32)
    for w in range(walkers):
        if w + ahead < walkers:
            tan_wait(w + ahead)
            group_sums(w + ahead)
            sums_copy(w + ahead).start()
        sums_copy(w).wait()
        n0 = spin[w].astype(F32)
        inv = 1.0 / jnp.concatenate(
            [jnp.full((1, 1, 1), n0, F32), jnp.full((1, 1, 1), elec - n0, F32)], 0
        )
        means = ((own_sums[w] + got_sums[w]) * inv).astype(BF16)
        mixed[...] = dot(means.reshape(2 * dirs, feat), w_spin[...]).reshape(2, dirs, feat)
        own_up = jnp.broadcast_to(own_columns[:, w : w + 1], (own, feat)) > 0.5
        own_slopes = slopes_s[0, w, pl.ds(off, own)]
        own_curve = slopes_s[1, w, pl.ds(off, own)]
        weighted = own_slopes * gain

        def product(i, to):
            d = pl.multiple_of(i * STAGE, STAGE)
            t = tan[w, pl.ds(d, STAGE)].reshape(STAGE * own, feat)
            to[...] = dot(t, w_self[...])

        def use(i, a, part, acc):
            for j in range(STAGE):
                d = i * STAGE + j
                m0 = mixed[0, pl.ds(d, 1)]
                m1 = mixed[1, pl.ds(d, 1)]
                ch = a[j * own : (j + 1) * own] + jnp.where(own_up, m0, m1)
                acc = acc + ch * ch
                p = (ch * weighted).reshape(own // 8, 8, feat).sum(axis=0)
                part[8 * j : 8 * j + 8] = p[:, :128] + p[:, 128:]
            for b in range(STAGE // 8):
                r = part[pl.ds(64 * b, 8, stride=8)]
                for k in range(1, 8):
                    r = r + part[pl.ds(64 * b + k, 8, stride=8)]
                partial[pl.ds(pl.multiple_of(i * STAGE + b * 8, 8), 8)] = r
            return acc

        stages = dirs // STAGE

        def step(i, acc):
            product(2 * i + 1, prod_b)
            acc = use(2 * i, prod_a, part_a, acc)
            product(jnp.minimum(2 * i + 2, stages - 1), prod_a)
            return use(2 * i + 1, prod_b, part_b, acc)

        product(0, prod_a)
        squares = lax.fori_loop(0, stages // 2, step, jnp.zeros((own, feat), F32))
        lap = own_slopes * lap_pre_s[w] + own_curve * squares
        lap_out[w] = lap
        lp = (lap * gain).reshape(own // 8, 8, feat).sum(axis=0)
        partial[dirs : dirs + 1] = jnp.sum(lp[:, :128] + lp[:, 128:], axis=0, keepdims=True)
        g = lax.dot_general(
            ones, partial[...], (((1,), (1,)), ((), ())),
            precision=lax.Precision.HIGHEST, preferred_element_type=F32,
        )
        own_ex[...] = jnp.where(iota((8, 256), 0) == w, g, own_ex[...])
    ex = to_partner(own_ex, got_ex, walkers + 2)
    ex.start()
    scatter_wait(shard_s, recv_s, 0)
    mine_s[...] = add_up(recv_s, XY)
    over_z(mine_s, zs, 0)
    ex.wait()
    both = own_ex[...] + got_ex[...]
    lane = iota((8, 256), 1)
    both = jnp.where(lane < dirs, both * both, jnp.where(lane == dirs, both, 0.0))
    pot = jnp.zeros((8, 1), F32)
    for w in range(walkers):
        pot = jnp.where(row81 == w, potential[w], pot)
    energy = -0.5 * jnp.sum(both, axis=1, keepdims=True) + pot
    diagonal = iota((8, 128), 0) == iota((8, 128), 1)
    energy_out[...] = jnp.sum(jnp.where(diagonal, energy, 0.0), axis=0, keepdims=True)
    esum = jnp.sum(energy, axis=0, keepdims=True)
    own_e[...] = jnp.broadcast_to(esum, (1, 128))
    scatter(own_e, plane_e, 3, whole=True)
    for c in range(2):
        grad = energy[0:1] * terms[0, :, c]
        for w in range(1, walkers):
            grad = grad + energy[w : w + 1] * terms[w, :, c]
        shard_e[c] = grad
        scatter(shard_e.at[c], recv_e.at[c], 1 + c)
    scatter_wait(own_e, plane_e, 3, whole=True)
    mine_z[...] = add_up(plane_e, XY)
    over_z(mine_z, all_e, 3)
    local = mine_z[:, :1] / (walkers * XY)
    for c in range(2):
        scatter_wait(shard_e.at[c], recv_e.at[c], 1 + c)
        mine_e[c] = (add_up(recv_e.at[c], XY) - local * mine_s[c]).astype(BF16)
        over_z(mine_e.at[c], ze.at[c], 1 + c)
    over_z_wait(mine_s, zs, 0)
    over_z_wait(mine_z, all_e, 3)
    center = add_up(all_e, NZ)[:, :1] / (walkers * XY * NZ)
    rest = jnp.zeros((2, 8, feat), F32)
    for j in range(NZ):
        rest = rest + (all_e[j, :, :1] / (walkers * XY) - center) * zs[j]

    def gather_copy(k, slot, c):
        return pltpu.make_async_remote_copy(
            src_ref=grads_out.at[core, c, here],
            dst_ref=grads_out.at[core, c, slot],
            send_sem=ag_send.at[c, k],
            recv_sem=ag_recv.at[c, k],
            device_id=(across(k)[0], core),
            device_id_type=MESH,
        )

    def hand_over(matrix, c):
        return pltpu.make_async_remote_copy(
            src_ref=grads_out.at[core, c],
            dst_ref=grads_out.at[matrix, c],
            send_sem=ag_send.at[c, 0],
            recv_sem=ag_recv.at[c, 0],
            device_id=partner,
            device_id_type=MESH,
        )

    for c in range(2):
        over_z_wait(mine_e.at[c], ze.at[c], 1 + c)
        grad = rest[c]
        for j in range(NZ):
            grad = grad + ze[c, j].astype(F32)
        grads_out[core, c, here] = grad.astype(BF16)
        for k in FAR_XY:
            gather_copy(k, here, c).start()
    for c in range(2):
        for k in FAR_XY:
            gather_copy(k, behind(k), c).wait()
        hand_over(core, c).start()
    for c in range(2):
        hand_over(1 - core, c).wait()


def results(lap, energy, grads, lap_out, energy_out, self_out, spin_out):
    lap_out[...] = lap[...]
    energy_out[...] = energy[0, : energy_out.shape[0]]
    for out, i in ((self_out, 0), (spin_out, 1)):
        halves = [grads[i, c].astype(F32)[:, None] for c in range(2)]
        out[...] = jnp.concatenate(halves, 1).reshape(out.shape)


def shards(
    values, lap_in, tangent, slot_electron, spin_up, w_self, w_spin, bias, readout, potential
):
    walkers, dirs, own, feat = tangent.shape
    elec = slot_electron.shape[1]
    per = feat // XY // 2
    vmem = pl.BlockSpec(memory_space=pltpu.VMEM)
    smem = pl.BlockSpec(memory_space=pltpu.SMEM)
    hbm = pl.BlockSpec(memory_space=pl.ANY)
    dma = pltpu.SemaphoreType.DMA
    lap, energy, grads = pl.pallas_call(
        body,
        out_shape=(
            jax.ShapeDtypeStruct((walkers, own, feat), F32),
            jax.ShapeDtypeStruct((1, 128), F32),
            jax.ShapeDtypeStruct((2, 2, XY, per, feat), BF16),
        ),
        in_specs=[hbm, hbm, hbm, hbm, smem, hbm, hbm, hbm, hbm, smem],
        out_specs=(vmem, vmem, vmem),
        scratch_shapes=[
            pltpu.VMEM((walkers, elec, feat), BF16),
            pltpu.VMEM((walkers, elec, feat), BF16),
            pltpu.VMEM((walkers, dirs, own, feat), BF16),
            pltpu.VMEM((walkers, 2, dirs, feat), F32),
            pltpu.VMEM((walkers, 2, dirs, feat), F32),
            pltpu.VMEM((2, dirs, feat), F32),
            pltpu.VMEM((walkers, 2 * BLOCK, BLOCK * own), BF16),
            pltpu.VMEM((walkers, XY, 2, per, feat), F32),
            pltpu.VMEM((2, walkers, elec, feat), F32),
            pltpu.VMEM((walkers, own, feat), F32),
            pltpu.VMEM((256, 128), F32),
            pltpu.VMEM((STAGE * own, feat), F32),
            pltpu.VMEM((STAGE * own, feat), F32),
            pltpu.VMEM((STAGE * 8 + 8, 128), F32),
            pltpu.VMEM((STAGE * 8 + 8, 128), F32),
            pltpu.VMEM((8, 256), F32),
            pltpu.VMEM((8, 256), F32),
            pltpu.VMEM((XY, 2, per, feat), F32),
            pltpu.VMEM((XY, 2, per, feat), F32),
            pltpu.VMEM((2, per, feat), F32),
            pltpu.VMEM((NZ, 2, per, feat), F32),
            pltpu.VMEM((2, XY, per, feat), F32),
            pltpu.VMEM((2, XY, per, feat), F32),
            pltpu.VMEM((2, per, feat), BF16),
            pltpu.VMEM((2, NZ, per, feat), BF16),
            pltpu.VMEM((1, 128), F32),
            pltpu.VMEM((XY, 1, 128), F32),
            pltpu.VMEM((1, 128), F32),
            pltpu.VMEM((NZ, 1, 128), F32),
            pltpu.VMEM((walkers, elec), jnp.int32),
            pltpu.VMEM((feat, feat), BF16),
            pltpu.VMEM((feat, feat), BF16),
            pltpu.VMEM((feat,), F32),
            pltpu.VMEM((feat,), F32),
            dma((7,)),
            dma((walkers,)),
            dma((walkers + 3,)),
            dma((walkers + 3,)),
            dma((4, XY)),
            dma((4, XY)),
            dma((4, NZ)),
            dma((4, NZ)),
            dma((2, XY)),
            dma((2, XY)),
        ],
        compiler_params=pltpu.CompilerParams(
            collective_id=0, has_side_effects=True, vmem_limit_bytes=60 << 20
        ),
        name="forward_laplacian",
    )(values, lap_in, tangent, slot_electron, spin_up, w_self, w_spin, bias, readout, potential)
    return pl.pallas_call(
        results,
        out_shape=(
            jax.ShapeDtypeStruct((walkers, own, feat), F32),
            jax.ShapeDtypeStruct((walkers,), F32),
            jax.ShapeDtypeStruct((feat, feat), F32),
            jax.ShapeDtypeStruct((feat, feat), F32),
        ),
        in_specs=[vmem, vmem, vmem],
        out_specs=(vmem, vmem, vmem, vmem),
        name="results",
    )(lap, energy, grads)


def solution(mesh):
    placed = (
        P("walk", "tan", None),
        P("walk", "tan", None),
        P("walk", None, "tan", None),
        P("walk", None),
        P("walk"),
        P(),
        P(),
        P(),
        P(),
        P("walk"),
    )
    return jax.shard_map(
        shards,
        mesh=mesh,
        in_specs=placed,
        out_specs=(P("walk", "tan", None), P("walk"), P(), P()),
        check_vma=False,
    )
```
